32 devices in a mesh: grp: 4 (over y, x), dp: 8 (over z, core).
Axes of the slice: x: 2, y: 2, z: 4, core: 2. Of those that a mesh axis runs over, the one named last changes fastest.
Arguments:
- hidden: bfloat16 [16384, 768], P(('grp', 'dp')), may hold values from -6 to 6
- weight: bfloat16 [768, 2048], P('dp'), may hold values from -1 to 1
- target: bfloat16 [16384, 2048], P(('grp', 'dp')), may hold values from -6 to 6
Outputs:
- hidden_grad: bfloat16 [16384, 768], P(('grp', 'dp'))
- combined: float32 [768, 2048], P('dp', 'grp')
The draws below stay inside these ranges and needn't reach their ends.
All inputs are finite; a program needn't handle non-finite values.
Results may differ from the reference program's by a relative error of at most 0.008.
Values may be sent and summed in bfloat16 or wider, within the bound.
A program may use at most 64 MiB of HBM per device.

```python
import math
import jax
import jax.numpy as jnp
from jax import lax

D = 2048
FF = 768
TOK_DEV = 512
TOKENS = 16384
N_GRP = 4
N_DP = 8


def draw_weight(key, part):
    key_scale = jax.random.fold_in(key, 11)
    key_values = jax.random.fold_in(key, 12)
    block_count = (FF + 23) // 24
    block_log = jax.random.uniform(key_scale, (block_count,), jnp.float32, -2.5, 0.5)
    row_scale = jnp.repeat(jnp.exp(block_log), 24)[:FF]
    values = jax.random.normal(key_values, (FF, D), jnp.float32)
    scaled = values * row_scale[:, None] * (1.0 / math.sqrt(FF))
    return jnp.clip(scaled, -1.0, 1.0).astype(jnp.bfloat16)


def draw_target(key, part):
    key_phase = jax.random.fold_in(key, 21)
    key_values = jax.random.fold_in(key, 22)
    phase = jax.random.uniform(key_phase, (), jnp.float32, 0.0, 1.0)
    position = jnp.arange(TOKENS).astype(jnp.float32) / float(TOKENS)
    low_log = math.log(0.15)
    high_log = math.log(3.0)
    middle = 0.5 * (low_log + high_log)
    half_span = 0.5 * (high_log - low_log)
    amplitude = jnp.exp(middle + half_span * jnp.sin(2.0 * math.pi * (position + phase)))
    values = jax.random.normal(key_values, (TOKENS, D), jnp.float32)
    return jnp.clip(values * amplitude[:, None], -6.0, 6.0).astype(jnp.bfloat16)


def steps_of(stream_key, shape, shards, low, top_value):
    gain = 1.0
    for dim, shards_of in shards:
        draws = jax.random.uniform(jax.random.fold_in(jax.random.fold_in(stream_key, 6), dim), (shards_of,), jnp.float32, low / len(shards), top_value / len(shards))
        gain = gain * jnp.repeat(jnp.exp(draws), shape[dim] // shards_of).reshape((-1,) + (1,) * (len(shape) - 1 - dim))
    return gain


def bell_draw(rng, shape, spread, most, split=(), kind=jnp.bfloat16):
    factor_of = steps_of(rng, shape, split, -0.22, 0.18) if split else 1.0
    entries = jax.random.normal(rng, shape, jnp.float32) * spread * factor_of
    return jnp.minimum(jnp.maximum(entries, -most), most).astype(kind)


def setup_inputs(seed: int = 0) -> dict:
    key_of = jax.random.split(jax.random.key(seed), 4)
    return {
        "hidden": bell_draw(key_of[0], (TOKENS, FF), 1.0, 6.0, ((0, 32),)),
        "weight": draw_weight(jax.random.fold_in(key_of[3], 71), 0),
        "target": draw_target(jax.random.fold_in(key_of[3], 71), 0),
    }


def adasum(first, second):
    eps = 1e-06
    own_sq = jnp.sum(first * first)
    other_sq = jnp.sum(second * second)
    cross = jnp.sum(first * second)
    return (1.0 - cross / (2.0 * (own_sq + eps))) * first + (1.0 - cross / (2.0 * (other_sq + eps))) * second

def reference(hidden, weight, target):
    factor = 1.0 / jnp.sqrt(jnp.float32(TOK_DEV * N_DP))
    hid_blocks = hidden.reshape(N_GRP, N_DP, TOK_DEV, FF)
    tgt_blocks = target.reshape(N_GRP, N_DP, TOK_DEV, D)

    def one_group(pair):
        hid_group, tgt_group = pair

        def one_member(total, member):
            hid_rows, tgt_rows = member
            output = jnp.dot(hid_rows, weight, preferred_element_type=jnp.float32)
            error = (output - tgt_rows.astype(jnp.float32)).astype(jnp.bfloat16)
            grad_rows = jnp.dot(error, weight.T, preferred_element_type=jnp.float32).astype(jnp.bfloat16)
            term = (jnp.dot(hid_rows.T, error, preferred_element_type=jnp.float32) * factor).astype(jnp.bfloat16)
            term = lax.optimization_barrier(term)
            return (total + term.astype(jnp.float32), grad_rows)
        start = jnp.zeros((FF, D), jnp.float32)
        total, grads = lax.scan(one_member, start, (hid_group, tgt_group))
        return (total, grads)
    vectors, hidden_grad = lax.map(one_group, (hid_blocks, tgt_blocks))
    count = N_GRP
    while count > 1:
        vectors = jax.vmap(adasum)(vectors[0::2], vectors[1::2])
        count = count // 2
    return (hidden_grad.reshape(TOKENS, FF), vectors[0])
```

```python
import functools
import math

import jax
import jax.numpy as jnp
from jax import lax
from jax.experimental import pallas as pl
from jax.experimental.pallas import tpu as pltpu
from jax.sharding import PartitionSpec as P

CORES = 2
EPS = 1e-06


def partner(value, axis, stride):
    mask = 2**stride
    pairs = [(source, source ^ mask) for source in range(lax.axis_size(axis))]
    return lax.ppermute(value, axis, pairs)


def coefficients(own_sq, other_sq, cross):
    return (1.0 - cross / (2.0 * (own_sq + EPS)), 1.0 - cross / (2.0 * (other_sq + EPS)))


def flip(value, other, size):
    result, bit = 0, 1
    while bit < size:
        result = result + ((value // bit + other // bit) % 2) * bit
        bit *= 2
    return result


def group_coefficients(gram, groups):
    def inner(left, right):
        total = 0.0
        for i, a in left.items():
            for j, b in right.items():
                total = total + a * b * gram[min(i, j), max(i, j)]
        return total

    vectors = [{i: 1.0} for i in range(groups)]
    while len(vectors) > 1:
        merged = []
        for first, second in zip(vectors[0::2], vectors[1::2]):
            own_sq = jnp.maximum(inner(first, first), 0.0)
            other_sq = jnp.maximum(inner(second, second), 0.0)
            coef_own, coef_other = coefficients(own_sq, other_sq, inner(first, second))
            both = {i: coef_own * a for i, a in first.items()}
            both.update({i: coef_other * b for i, b in second.items()})
            merged.append(both)
        vectors = merged
    return vectors[0]


def kernel(
    groups,
    members,
    factor,
    hid_ref,
    wsh_ref,
    tgt_ref,
    hg_ref,
    comb_ref,
    hid_t,
    w_all,
    term,
    pair,
    hop_in,
    hop_out,
    v_out,
    gath,
    gram_all,
    gram_far,
    gram_sum,
    c_out,
    c_in,
    acc,
    zs,
    zr,
    xs,
    xr,
    ss,
    sr,
    s2,
    r2,
    hs,
    hr,
    vs,
    vr,
    gs,
    gr,
    cs,
    cr,
):
    depth = members // CORES
    half = depth // 2
    rows, width = wsh_ref.shape
    cols = width // groups
    ff = rows * members
    g = lax.axis_index("grp")
    d = lax.axis_index("dp")
    z = d // CORES
    c = d % CORES
    sib = 1 - c

    def copy(src, dst, send, recv, grp, dp):
        return pltpu.make_async_remote_copy(
            src_ref=src,
            dst_ref=dst,
            send_sem=send,
            recv_sem=recv,
            device_id=(grp, dp),
            device_id_type=pl.DeviceIdType.MESH,
        )

    def col(m):
        return pl.ds(pl.multiple_of(flip(g, m, groups) * cols, 128), cols)

    barrier = pltpu.get_barrier_semaphore()
    peers = [(g, flip(z, k, depth) * CORES + c) for k in range(1, depth)]
    peers += [(flip(g, m, groups), d) for m in range(1, groups)]
    peers += [(flip(g, m, groups), z * CORES + sib) for m in range(groups)]
    for grp, dp in peers:
        pl.semaphore_signal(
            barrier, inc=1, device_id=(grp, dp), device_id_type=pl.DeviceIdType.MESH
        )
    pl.semaphore_wait(barrier, len(peers))

    def z_copy(k):
        return copy(
            wsh_ref.at[:, col(0)],
            w_all.at[0, d],
            zs.at[k],
            zr.at[k],
            g,
            flip(z, k, depth) * CORES + c,
        )

    def own_copy(m):
        return copy(
            wsh_ref.at[:, col(m)], w_all.at[m, d], ss.at[m, 0], sr.at[m, 0], g, z * CORES + sib
        )

    def x_copy(m, k):
        row = flip(z, k, depth) * CORES + c
        return copy(
            w_all.at[0, row], w_all.at[m, row], xs.at[m, k], xr.at[m, k], flip(g, m, groups), d
        )

    def s_copy(m, k):
        row = flip(z, k, depth) * CORES + c
        return copy(
            w_all.at[m, row], w_all.at[m, row], ss.at[m, k], sr.at[m, k], g, z * CORES + sib
        )

    for k in range(1, depth):
        z_copy(k).start()
    for m in range(groups):
        own_copy(m).start()
    for m in range(groups):
        w_all[m, d] = wsh_ref[:, col(m)]
    hid_t[...] = hid_ref[...].T

    for k in range(1, depth):
        z_copy(k).wait_recv()
        s_copy(0, k).start()
        for m in range(1, groups):
            x_copy(m, k).start()

    def pair_copy(s):
        return copy(
            term.at[s, sib], pair.at[s], s2.at[s], r2.at[s], g, z * CORES + sib
        )

    def hop_copy(s, way, j):
        target = z - 1 if way == 0 else z + 1
        return copy(
            hop_out.at[s, way, j],
            hop_in.at[s, way, j],
            hs.at[s, way, j],
            hr.at[s, way, j],
            g,
            target * CORES + c,
        )

    def v_copy(s, j):
        return copy(
            v_out.at[s, j], gath.at[g, j], vs.at[s, j], vr.at[s, j], flip(g, s, groups), d
        )

    def chip_sum(s, block):
        return term[s, c, block].astype(jnp.float32) + pair[s, block].astype(jnp.float32)

    def process(t):
        for way in range(2):
            place = depth - 1 - z if way == 0 else z
            s = t - place
            inside = (s >= 0) & (s < groups)

            @pl.when(inside & (place == 0))
            def _():
                for j in range(half):
                    hop_out[s, way, j] = chip_sum(s, way * half + j).astype(jnp.bfloat16)
                    hop_copy(s, way, j).start()

            @pl.when(inside & (place > 0) & (place < depth - 1))
            def _():
                for j in range(half):
                    hop_copy(s, way, j).wait_recv()
                    total = chip_sum(s, way * half + j) + hop_in[s, way, j].astype(jnp.float32)
                    hop_out[s, way, j] = total.astype(jnp.bfloat16)
                    hop_copy(s, way, j).start()

            @pl.when(inside & (place == depth - 1))
            def _():
                for j in range(half):
                    hop_copy(s, way, j).wait_recv()
                    total = chip_sum(s, way * half + j) + hop_in[s, way, j].astype(jnp.float32)
                    final = total.astype(jnp.bfloat16)

                    @pl.when(s == 0)
                    def _():
                        gath[g, j] = final

                    @pl.when(s > 0)
                    def _():
                        v_out[s, j] = final
                        v_copy(s, j).start()

    def slot(m, carry):
        @pl.when(m > 0)
        def _():
            for k in range(1, depth):
                x_copy(m, k).wait_recv()
                s_copy(m, k).start()

        for k in range(depth):
            s_copy(m, k).wait_recv()
        weight = w_all[m].reshape(ff, cols)
        output = jnp.dot(hid_ref[...], weight, preferred_element_type=jnp.float32)
        error = (output - tgt_ref[:, col(m)].astype(jnp.float32)).astype(jnp.bfloat16)
        product = jnp.dot(hid_t[...], error, preferred_element_type=jnp.float32)
        product = (product * factor).astype(jnp.bfloat16)
        for i in range(members):
            term[m, i % CORES, i // CORES] = product[i * rows : (i + 1) * rows]
        pair_copy(m).start()
        grad = lax.dot_general(
            error, weight, (((1,), (1,)), ((), ())), preferred_element_type=jnp.float32
        )

        @pl.when(m == 0)
        def _():
            acc[...] = grad

        @pl.when(m > 0)
        def _():
            acc[...] += grad

        pair_copy(m).wait_recv()
        process(m)
        return carry

    lax.fori_loop(0, groups, slot, 0)
    hg_ref[...] = acc[...].astype(jnp.bfloat16)

    def tail(t, carry):
        process(t)
        return carry

    lax.fori_loop(groups, groups + depth - 1, tail, 0)

    is_end = (z == 0) | (z == depth - 1)
    pairs = [(i, j) for i in range(groups) for j in range(i, groups)]
    near = [(m, e) for m in range(groups) for e in range(CORES) if m + e > 0]
    far = (depth - 1 - z) * CORES + c

    def near_copy(n):
        m, e = near[n]
        core = c if e == 0 else sib
        return copy(
            gram_sum.at[0],
            gram_all.at[n],
            gs.at[n],
            gr.at[n],
            flip(g, m, groups),
            z * CORES + core,
        )

    def far_copy():
        return copy(gram_sum.at[1], gram_far, gs.at[len(near)], gr.at[len(near)], g, far)

    def c_copy(j, target):
        return copy(c_out.at[j], c_in, cs.at[j], cr.at[0], g, target * CORES + c)

    @pl.when(is_end)
    def _():
        for s in range(1, groups):
            for j in range(half):
                v_copy(s, j).wait_recv()
        vecs = [gath[i].reshape(half * rows, cols).astype(jnp.float32) for i in range(groups)]
        lines = []
        for i, j in pairs:
            line = jnp.sum(vecs[i] * vecs[j], axis=0, keepdims=True)
            lines.append(sum(line[:, n * 128 : (n + 1) * 128] for n in range(cols // 128)))
        pad = gram_sum.shape[1] - len(lines)
        lines.append(jnp.zeros((pad, 128), jnp.float32))
        mine = jnp.concatenate(lines, axis=0)
        gram_sum[0] = mine
        for n in range(len(near)):
            near_copy(n).start()
        for n in range(len(near)):
            near_copy(n).wait_recv()
        mine = mine + jnp.sum(gram_all[...], axis=0)
        gram_sum[1] = mine
        far_copy().start()
        far_copy().wait_recv()
        total = jnp.sum(mine + gram_far[...], axis=1, keepdims=True)
        gram = {ij: total[n : n + 1] for n, ij in enumerate(pairs)}
        coef = group_coefficients(gram, groups)
        for j in range(half):
            mixed = sum(coef[i] * gath[i, j].astype(jnp.float32) for i in range(groups))
            for way in range(2):
                target = way * half + j

                @pl.when(z == way * (depth - 1))
                def _():
                    if target == way * (depth - 1):
                        comb_ref[...] = mixed
                    else:
                        c_out[j] = mixed.astype(jnp.bfloat16)
                        c_copy(j, target).start()

        for s in range(1, groups):
            for j in range(half):
                v_copy(s, j).wait_send()
        for n in range(len(near)):
            near_copy(n).wait_send()
        far_copy().wait_send()
        for j in range(half):
            for way in range(2):
                target = way * half + j
                if target != way * (depth - 1):

                    @pl.when(z == way * (depth - 1))
                    def _():
                        c_copy(j, target).wait_send()

    @pl.when(jnp.logical_not(is_end))
    def _():
        c_copy(0, 0).wait_recv()
        comb_ref[...] = c_in[...].astype(jnp.float32)

    for k in range(1, depth):
        z_copy(k).wait_send()
        for m in range(1, groups):
            x_copy(m, k).wait_send()
    for m in range(groups):
        pair_copy(m).wait_send()
        for k in range(depth):
            s_copy(m, k).wait_send()
        for way in range(2):

            @pl.when(z != way * (depth - 1))
            def _():
                for j in range(half):
                    hop_copy(m, way, j).wait_send()


def fused(hidden, weight, target):
    groups = lax.axis_size("grp")
    members = lax.axis_size("dp")
    tokens, ff = hidden.shape
    rows, width = weight.shape
    cols = width // groups
    depth = members // CORES
    half = depth // 2
    factor = 1.0 / math.sqrt(tokens * members)
    bf16, f32 = jnp.bfloat16, jnp.float32
    pads = -(-(groups * (groups + 1) // 2) // 8) * 8 + 8
    near = groups * CORES - 1
    vmem = pl.BlockSpec(memory_space=pltpu.VMEM)
    dma = pltpu.SemaphoreType.DMA
    block = (rows, cols)
    scratch = [
        pltpu.VMEM((ff, tokens), bf16),
        pltpu.VMEM((groups, members) + block, bf16),
        pltpu.VMEM((groups, CORES, depth) + block, bf16),
        pltpu.VMEM((groups, depth) + block, bf16),
        pltpu.VMEM((groups, 2, half) + block, bf16),
        pltpu.VMEM((groups, 2, half) + block, bf16),
        pltpu.VMEM((groups, half) + block, bf16),
        pltpu.VMEM((groups, half) + block, bf16),
        pltpu.VMEM((near, pads, 128), f32),
        pltpu.VMEM((pads, 128), f32),
        pltpu.VMEM((2, pads, 128), f32),
        pltpu.VMEM((half,) + block, bf16),
        pltpu.VMEM(block, bf16),
        pltpu.VMEM((tokens, ff), f32),
        dma((depth,)),
        dma((depth,)),
        dma((groups, depth)),
        dma((groups, depth)),
        dma((groups, depth)),
        dma((groups, depth)),
        dma((groups,)),
        dma((groups,)),
        dma((groups, 2, half)),
        dma((groups, 2, half)),
        dma((groups, half)),
        dma((groups, half)),
        dma((near + 1,)),
        dma((near + 1,)),
        dma((half,)),
        dma((1,)),
    ]
    return pl.pallas_call(
        functools.partial(kernel, groups, members, factor),
        out_shape=(
            jax.ShapeDtypeStruct((tokens, ff), bf16),
            jax.ShapeDtypeStruct(block, f32),
        ),
        in_specs=[vmem] * 3,
        out_specs=(vmem, vmem),
        scratch_shapes=scratch,
        compiler_params=pltpu.CompilerParams(
            collective_id=0, has_side_effects=True, vmem_limit_bytes=56 * 2**20
        ),
    )(hidden, weight, target)


def plain(hidden, weight, target):
    rows = hidden.shape[0]
    members = lax.axis_size("dp")
    factor = 1.0 / math.sqrt(rows * members)
    weight_full = lax.all_gather(weight, "dp", axis=0, tiled=True)
    output = jnp.dot(hidden, weight_full, preferred_element_type=jnp.float32)
    error = (output - target.astype(jnp.float32)).astype(jnp.bfloat16)
    product = lax.dot_general(
        hidden, error, (((0,), (0,)), ((), ())), preferred_element_type=jnp.float32
    )
    shard = lax.psum_scatter(
        (product * factor).astype(jnp.bfloat16), "dp", scatter_dimension=0, tiled=True
    ).astype(jnp.float32)
    hidden_grad = lax.dot_general(
        error, weight_full, (((1,), (1,)), ((), ())), preferred_element_type=jnp.float32
    ).astype(jnp.bfloat16)
    levels = lax.axis_size("grp").bit_length() - 1
    for level in range(levels):
        other = partner(shard.astype(jnp.bfloat16), "grp", level).astype(shard.dtype)
        own_sq, other_sq, cross = lax.psum(
            (jnp.sum(shard * shard), jnp.sum(other * other), jnp.sum(shard * other)), "dp"
        )
        coef_own, coef_other = coefficients(own_sq, other_sq, cross)
        shard = coef_own * shard + coef_other * other
    columns = shard.shape[1] // lax.axis_size("grp")
    mine = lax.dynamic_slice_in_dim(shard, lax.axis_index("grp") * columns, columns, 1)
    return (hidden_grad, mine)


def shards(hidden, weight, target):
    groups, members = lax.axis_size("grp"), lax.axis_size("dp")
    rows, width = weight.shape
    power = all(n & (n - 1) == 0 for n in (groups, members))
    aligned = rows % 16 == 0 and width % (128 * groups) == 0
    if power and aligned and members >= 2 * CORES and groups > 1:
        return fused(hidden, weight, target)
    return plain(hidden, weight, target)


def solution(mesh):
    in_specs = (P(("grp", "dp"), None), P("dp", None), P(("grp", "dp"), None))
    out_specs = (P(("grp", "dp"), None), P("dp", "grp"))
    return jax.shard_map(shards, mesh=mesh, in_specs=in_specs, out_specs=out_specs, check_vma=False)
```

```python
import functools
import math

import jax
import jax.numpy as jnp
from jax import lax
from jax.experimental import pallas as pl
from jax.experimental.pallas import tpu as pltpu
from jax.sharding import PartitionSpec as P

CORES = 2
PARTS = 2
EPS = 1e-06


def partner(value, axis, stride):
    mask = 2**stride
    pairs = [(source, source ^ mask) for source in range(lax.axis_size(axis))]
    return lax.ppermute(value, axis, pairs)


def coefficients(own_sq, other_sq, cross):
    return (1.0 - cross / (2.0 * (own_sq + EPS)), 1.0 - cross / (2.0 * (other_sq + EPS)))


def flip(value, other, size):
    result, bit = 0, 1
    while bit < size:
        result = result + ((value // bit + other // bit) % 2) * bit
        bit *= 2
    return result


def group_coefficients(gram, groups):
    def inner(left, right):
        total = 0.0
        for i, a in left.items():
            for j, b in right.items():
                total = total + a * b * gram[min(i, j), max(i, j)]
        return total

    vectors = [{i: 1.0} for i in range(groups)]
    while len(vectors) > 1:
        merged = []
        for first, second in zip(vectors[0::2], vectors[1::2]):
            own_sq = jnp.maximum(inner(first, first), 0.0)
            other_sq = jnp.maximum(inner(second, second), 0.0)
            coef_own, coef_other = coefficients(own_sq, other_sq, inner(first, second))
            both = {i: coef_own * a for i, a in first.items()}
            both.update({i: coef_other * b for i, b in second.items()})
            merged.append(both)
        vectors = merged
    return vectors[0]


def kernel(
    groups,
    members,
    factor,
    hid_hbm,
    wsh_ref,
    tgt_hbm,
    hg_hbm,
    comb_ref,
    hid_ref,
    tgt_ref,
    hg_ref,
    hid_t,
    w_all,
    term,
    pair,
    hop_in,
    hop_out,
    v_out,
    gath,
    gram_all,
    gram_far,
    gram_sum,
    acc,
    zs,
    zr,
    xs,
    xr,
    ds,
    dr,
    ss,
    sr,
    s2,
    r2,
    hs,
    hr,
    vs,
    vr,
    gs,
    gr,
    ms,
    mr,
    fs,
    fr,
    local,
):
    depth = members // CORES
    half = depth // 2
    rows, width = wsh_ref.shape
    cols = width // groups
    ff = rows * members
    g = lax.axis_index("grp")
    d = lax.axis_index("dp")
    z = d // CORES
    c = d % CORES
    sib = 1 - c
    is_end = (z == 0) | (z == depth - 1)
    end = z // (depth - 1)
    held = end * (half - 1)

    def part(p):
        return pl.ds(p * (rows // PARTS), rows // PARTS)


    def copy(src, dst, send, recv, grp, dp):
        return pltpu.make_async_remote_copy(
            src_ref=src,
            dst_ref=dst,
            send_sem=send,
            recv_sem=recv,
            device_id=(grp, dp),
            device_id_type=pl.DeviceIdType.MESH,
        )

    def col(m):
        return pl.ds(pl.multiple_of(flip(g, m, groups) * cols, 128), cols)

    hid_load = pltpu.make_async_copy(hid_hbm, hid_ref, local.at[0])
    tgt_load = pltpu.make_async_copy(tgt_hbm, tgt_ref, local.at[1])
    hg_store = pltpu.make_async_copy(hg_ref, hg_hbm, local.at[2])

    def own_load(m):
        return pltpu.make_async_copy(wsh_ref.at[:, col(m)], w_all.at[m, d], local.at[3 + m])

    barrier = pltpu.get_barrier_semaphore()
    peers = [(g, flip(z, k, depth) * CORES + c) for k in range(1, depth)]
    peers += [(flip(g, m, groups), d) for m in range(1, groups)]
    peers += [(flip(g, m, groups), z * CORES + sib) for m in range(groups)]
    for grp, dp in peers:
        pl.semaphore_signal(
            barrier, inc=1, device_id=(grp, dp), device_id_type=pl.DeviceIdType.MESH
        )
    pl.semaphore_wait(barrier, len(peers))

    def z_copy(src, way, block):
        target = z - 1 if way == 0 else z + 1
        row = src * CORES + c
        return copy(
            block, w_all.at[0, row], zs.at[way, src], zr.at[src], g, target * CORES + c
        )

    def own_copy(m):
        return copy(
            wsh_ref.at[:, col(m)], w_all.at[m, d], ss.at[m, z], sr.at[m, z], g, z * CORES + sib
        )

    def x_copy(m, src):
        row = src * CORES + c
        return copy(
            w_all.at[0, row], w_all.at[m, row], xs.at[m, src], xr.at[m, src], flip(g, m, groups), d
        )

    def d_copy(side, src):
        side_rows = pl.ds(side * (rows // 2), rows // 2)
        row = src * CORES + c
        return copy(
            w_all.at[1 + side, row, side_rows],
            w_all.at[3, row, side_rows],
            ds.at[side, src],
            dr.at[side, src],
            flip(g, 2 - side, groups),
            d,
        )

    def s_copy(m, src):
        row = src * CORES + c
        return copy(
            w_all.at[m, row], w_all.at[m, row], ss.at[m, src], sr.at[m, src], g, z * CORES + sib
        )

    def at_distance(h, action):
        for way in range(2):
            src = z + h if way == 0 else z - h

            @pl.when((src >= 0) & (src < depth))
            def _():
                action(src, way)

    def sends_on(way):
        return z > 0 if way == 0 else z < depth - 1

    def line_step(src, way):
        z_copy(src, way, wsh_ref.at[:, col(0)]).wait_recv()

        @pl.when(sends_on(way))
        def _():
            z_copy(src, way, w_all.at[0, src * CORES + c]).start()

        x_copy(1, src).start()
        x_copy(2, src).start()
        s_copy(0, src).start()

    def cross_step(src, way):
        for m in (1, 2):
            x_copy(m, src).wait_recv()
            d_copy(m - 1, src).start()
            s_copy(m, src).start()

    def corner_step(src, way):
        for side in range(2):
            d_copy(side, src).wait_recv()
        s_copy(3, src).start()

    for way in range(2):

        @pl.when(sends_on(way))
        def _():
            z_copy(z, way, wsh_ref.at[:, col(0)]).start()

    for m in range(groups):
        own_copy(m).start()
    for m in range(groups):
        own_load(m).start()
    hid_load.start()
    tgt_load.start()
    hid_load.wait()
    hid_t[...] = hid_ref[...].T

    for h in range(1, depth):
        at_distance(h, line_step)
        if 1 <= h - 1 < depth - 2:
            at_distance(h - 1, cross_step)
    tgt_load.wait()
    for m in range(groups):
        own_load(m).wait()

    def pair_copy(s):
        return copy(
            term.at[s, sib], pair.at[s], s2.at[s], r2.at[s], g, z * CORES + sib
        )

    def hop_copy(s, way, j, p):
        target = z - 1 if way == 0 else z + 1
        return copy(
            hop_out.at[s, way, j, part(p)],
            hop_in.at[s, way, j, part(p)],
            hs.at[s, way, j, p],
            hr.at[s, way, j, p],
            g,
            target * CORES + c,
        )

    def v_copy(s, j, p):
        return copy(
            v_out.at[s, j, part(p)],
            gath.at[g, j, part(p)],
            vs.at[s, j, p],
            vr.at[s, j, p],
            flip(g, s, groups),
            d,
        )

    def m_copy(s, j):
        group = flip(g, s, groups)
        return copy(
            gath.at[group, j],
            gath.at[group, 0],
            ms.at[s, j],
            mr.at[s],
            g,
            (end * half + j) * CORES + c,
        )

    def pieces():
        return [(j, p) for j in range(half) for p in range(PARTS)]

    def to_middle(action):
        for j in range(half):

            @pl.when(j != held)
            def _():
                action(j)

    def forward(s):
        @pl.when(s > 0)
        def _():
            for j, p in pieces():
                v_copy(s, j, p).wait_recv()

        to_middle(lambda j: m_copy(s, j).start())

    def chip_sum(s, block, p):
        return term[s, c, block, part(p)].astype(jnp.float32) + pair[s, block, part(p)].astype(
            jnp.float32
        )

    def process(t):
        for way in range(2):
            place = depth - 1 - z if way == 0 else z
            s = t - place
            inside = (s >= 0) & (s < groups)

            @pl.when(inside & (place == 0))
            def _():
                for j, p in pieces():
                    mine = chip_sum(s, way * half + j, p)
                    hop_out[s, way, j, part(p)] = mine.astype(jnp.bfloat16)
                    hop_copy(s, way, j, p).start()

            @pl.when(inside & (place > 0) & (place < depth - 1))
            def _():
                for j, p in pieces():
                    mine = chip_sum(s, way * half + j, p)
                    hop_copy(s, way, j, p).wait_recv()
                    total = mine + hop_in[s, way, j, part(p)].astype(jnp.float32)
                    hop_out[s, way, j, part(p)] = total.astype(jnp.bfloat16)
                    hop_copy(s, way, j, p).start()

            @pl.when(inside & (place == depth - 1))
            def _():
                for j, p in pieces():
                    mine = chip_sum(s, way * half + j, p)
                    hop_copy(s, way, j, p).wait_recv()
                    total = mine + hop_in[s, way, j, part(p)].astype(jnp.float32)
                    final = total.astype(jnp.bfloat16)

                    @pl.when(s == 0)
                    def _():
                        gath[g, j, part(p)] = final

                    @pl.when(s > 0)
                    def _():
                        v_out[s, j, part(p)] = final
                        v_copy(s, j, p).start()

        s1 = t - depth

        @pl.when(is_end & (s1 >= 0) & (s1 < groups - 1))
        def _():
            forward(s1)

    def slot(m, carry):
        @pl.when(m == 1)
        def _():
            for h in range(max(1, depth - 2), depth):
                at_distance(h, cross_step)

        @pl.when(m == 2)
        def _():
            for h in range(1, depth):
                at_distance(h, corner_step)

        for k in range(depth):
            s_copy(m, k).wait_recv()
        weight = w_all[m].reshape(ff, cols)
        output = jnp.dot(hid_ref[...], weight, preferred_element_type=jnp.float32)
        error = (output - tgt_ref[:, col(m)].astype(jnp.float32)).astype(jnp.bfloat16)
        product = jnp.dot(hid_t[...], error, preferred_element_type=jnp.float32)
        product = (product * factor).astype(jnp.bfloat16)
        for i in range(members):
            term[m, i % CORES, i // CORES] = product[i * rows : (i + 1) * rows]
        pair_copy(m).start()
        grad = lax.dot_general(
            error, weight, (((1,), (1,)), ((), ())), preferred_element_type=jnp.float32
        )

        @pl.when(m == 0)
        def _():
            acc[...] = grad

        @pl.when(m > 0)
        def _():
            acc[...] += grad

        pair_copy(m).wait_recv()
        process(m)
        return carry

    lax.fori_loop(0, groups, slot, 0)
    hg_ref[...] = acc[...].astype(jnp.bfloat16)
    hg_store.start()

    def tail(t, carry):
        process(t)
        return carry

    lax.fori_loop(groups, groups + depth - 1, tail, 0)

    pairs = [(i, j) for i in range(groups) for j in range(i, groups)]
    near = [(m, e) for m in range(groups) for e in range(CORES) if m + e > 0]

    def near_copy(n):
        m, e = near[n]
        core = c if e == 0 else sib
        return copy(
            gram_sum,
            gram_all.at[n],
            gs.at[n],
            gr.at[n],
            flip(g, m, groups),
            z * CORES + core,
        )

    def far_copy(k, e):
        return copy(
            gram_far.at[e],
            gram_far.at[e],
            fs.at[k],
            fr.at[e],
            g,
            flip(z, k, depth) * CORES + c,
        )

    @pl.when(is_end)
    def _():
        forward(groups - 1)
        vecs = [gath[i].reshape(half * rows, cols).astype(jnp.float32) for i in range(groups)]
        lines = []
        for i, j in pairs:
            line = jnp.sum(vecs[i] * vecs[j], axis=0, keepdims=True)
            lines.append(sum(line[:, n * 128 : (n + 1) * 128] for n in range(cols // 128)))
        pad = gram_sum.shape[0] - len(lines)
        lines.append(jnp.zeros((pad, 128), jnp.float32))
        mine = jnp.concatenate(lines, axis=0)
        gram_sum[...] = mine
        for n in range(len(near)):
            near_copy(n).start()
        for n in range(len(near)):
            near_copy(n).wait_recv()
        gram_far[end] = mine + jnp.sum(gram_all[...], axis=0)
        for k in range(1, depth):
            far_copy(k, end).start()
        far_copy(1, 1 - end).wait_recv()

    @pl.when(jnp.logical_not(is_end))
    def _():
        for s in range(groups):
            m_copy(s, 0).wait_recv()
        for e in range(2):
            far_copy(1, e).wait_recv()

    total = jnp.sum(gram_far[0] + gram_far[1], axis=1, keepdims=True)
    gram = {ij: total[n : n + 1] for n, ij in enumerate(pairs)}
    coef = group_coefficients(gram, groups)
    comb_ref[...] = sum(coef[i] * gath[i, held].astype(jnp.float32) for i in range(groups))

    @pl.when(is_end)
    def _():
        for s in range(1, groups):
            for j, p in pieces():
                v_copy(s, j, p).wait_send()
        for s in range(groups):
            to_middle(lambda j: m_copy(s, j).wait_send())
        for n in range(len(near)):
            near_copy(n).wait_send()
        for k in range(1, depth):
            far_copy(k, end).wait_send()

    for way in range(2):
        for h in range(depth):
            src = z - h if way else z + h

            @pl.when(sends_on(way) & (src >= 0) & (src < depth))
            def _():
                z_copy(src, way, wsh_ref.at[:, col(0)]).wait_send()

    def cross_done(src, way):
        for m in (1, 2):
            x_copy(m, src).wait_send()
            d_copy(m - 1, src).wait_send()

    for h in range(1, depth):
        at_distance(h, cross_done)
    hg_store.wait()
    for m in range(groups):
        pair_copy(m).wait_send()
        for k in range(depth):
            s_copy(m, k).wait_send()
        for way in range(2):

            @pl.when(z != way * (depth - 1))
            def _():
                for j, p in pieces():
                    hop_copy(m, way, j, p).wait_send()


def fused(hidden, weight, target):
    groups = lax.axis_size("grp")
    members = lax.axis_size("dp")
    tokens, ff = hidden.shape
    rows, width = weight.shape
    cols = width // groups
    depth = members // CORES
    half = depth // 2
    factor = 1.0 / math.sqrt(tokens * members)
    bf16, f32 = jnp.bfloat16, jnp.float32
    pads = -(-(groups * (groups + 1) // 2) // 8) * 8 + 8
    near = groups * CORES - 1
    vmem = pl.BlockSpec(memory_space=pltpu.VMEM)
    hbm = pl.BlockSpec(memory_space=pltpu.HBM)
    dma = pltpu.SemaphoreType.DMA
    block = (rows, cols)
    scratch = [
        pltpu.VMEM((tokens, ff), bf16),
        pltpu.VMEM((tokens, width), bf16),
        pltpu.VMEM((tokens, ff), bf16),
        pltpu.VMEM((ff, tokens), bf16),
        pltpu.VMEM((groups, members) + block, bf16),
        pltpu.VMEM((groups, CORES, depth) + block, bf16),
        pltpu.VMEM((groups, depth) + block, bf16),
        pltpu.VMEM((groups, 2, half) + block, bf16),
        pltpu.VMEM((groups, 2, half) + block, bf16),
        pltpu.VMEM((groups, half) + block, bf16),
        pltpu.VMEM((groups, half) + block, bf16),
        pltpu.VMEM((near, pads, 128), f32),
        pltpu.VMEM((2, pads, 128), f32),
        pltpu.VMEM((pads, 128), f32),
        pltpu.VMEM((tokens, ff), f32),
        dma((2, depth)),
        dma((depth,)),
        dma((groups, depth)),
        dma((groups, depth)),
        dma((2, depth)),
        dma((2, depth)),
        dma((groups, depth)),
        dma((groups, depth)),
        dma((groups,)),
        dma((groups,)),
        dma((groups, 2, half, PARTS)),
        dma((groups, 2, half, PARTS)),
        dma((groups, half, PARTS)),
        dma((groups, half, PARTS)),
        dma((near,)),
        dma((near,)),
        dma((groups, half)),
        dma((groups,)),
        dma((depth,)),
        dma((2,)),
        dma((3 + groups,)),
    ]
    return pl.pallas_call(
        functools.partial(kernel, groups, members, factor),
        out_shape=(
            jax.ShapeDtypeStruct((tokens, ff), bf16),
            jax.ShapeDtypeStruct(block, f32),
        ),
        in_specs=[hbm] * 3,
        out_specs=(hbm, vmem),
        scratch_shapes=scratch,
        compiler_params=pltpu.CompilerParams(
            collective_id=0, has_side_effects=True, vmem_limit_bytes=56 * 2**20
        ),
    )(hidden, weight, target)


def plain(hidden, weight, target):
    rows = hidden.shape[0]
    members = lax.axis_size("dp")
    factor = 1.0 / math.sqrt(rows * members)
    weight_full = lax.all_gather(weight, "dp", axis=0, tiled=True)
    output = jnp.dot(hidden, weight_full, preferred_element_type=jnp.float32)
    error = (output - target.astype(jnp.float32)).astype(jnp.bfloat16)
    product = lax.dot_general(
        hidden, error, (((0,), (0,)), ((), ())), preferred_element_type=jnp.float32
    )
    shard = lax.psum_scatter(
        (product * factor).astype(jnp.bfloat16), "dp", scatter_dimension=0, tiled=True
    ).astype(jnp.float32)
    hidden_grad = lax.dot_general(
        error, weight_full, (((1,), (1,)), ((), ())), preferred_element_type=jnp.float32
    ).astype(jnp.bfloat16)
    levels = lax.axis_size("grp").bit_length() - 1
    for level in range(levels):
        other = partner(shard.astype(jnp.bfloat16), "grp", level).astype(shard.dtype)
        own_sq, other_sq, cross = lax.psum(
            (jnp.sum(shard * shard), jnp.sum(other * other), jnp.sum(shard * other)), "dp"
        )
        coef_own, coef_other = coefficients(own_sq, other_sq, cross)
        shard = coef_own * shard + coef_other * other
    columns = shard.shape[1] // lax.axis_size("grp")
    mine = lax.dynamic_slice_in_dim(shard, lax.axis_index("grp") * columns, columns, 1)
    return (hidden_grad, mine)


def shards(hidden, weight, target):
    groups, members = lax.axis_size("grp"), lax.axis_size("dp")
    rows, width = weight.shape
    power = all(n & (n - 1) == 0 for n in (groups, members))
    aligned = rows % (16 * PARTS) == 0 and width % (128 * groups) == 0
    if power and aligned and members >= 2 * CORES and groups == 4:
        return fused(hidden, weight, target)
    return plain(hidden, weight, target)


def solution(mesh):
    in_specs = (P(("grp", "dp"), None), P("dp", None), P(("grp", "dp"), None))
    out_specs = (P(("grp", "dp"), None), P("dp", "grp"))
    return jax.shard_map(shards, mesh=mesh, in_specs=in_specs, out_specs=out_specs, check_vma=False)
```

```python
import functools
import math

import jax
import jax.numpy as jnp
from jax import lax
from jax.experimental import pallas as pl
from jax.experimental.pallas import tpu as pltpu
from jax.sharding import PartitionSpec as P

CORES = 2
PARTS = 2
EPS = 1e-06


def partner(value, axis, stride):
    mask = 2**stride
    pairs = [(source, source ^ mask) for source in range(lax.axis_size(axis))]
    return lax.ppermute(value, axis, pairs)


def coefficients(own_sq, other_sq, cross):
    return (1.0 - cross / (2.0 * (own_sq + EPS)), 1.0 - cross / (2.0 * (other_sq + EPS)))


def flip(value, other, size):
    result, bit = 0, 1
    while bit < size:
        result = result + ((value // bit + other // bit) % 2) * bit
        bit *= 2
    return result


def group_coefficients(gram, groups):
    def inner(left, right):
        total = 0.0
        for i, a in left.items():
            for j, b in right.items():
                total = total + a * b * gram[min(i, j), max(i, j)]
        return total

    vectors = [{i: 1.0} for i in range(groups)]
    while len(vectors) > 1:
        merged = []
        for first, second in zip(vectors[0::2], vectors[1::2]):
            own_sq = jnp.maximum(inner(first, first), 0.0)
            other_sq = jnp.maximum(inner(second, second), 0.0)
            coef_own, coef_other = coefficients(own_sq, other_sq, inner(first, second))
            both = {i: coef_own * a for i, a in first.items()}
            both.update({i: coef_other * b for i, b in second.items()})
            merged.append(both)
        vectors = merged
    return vectors[0]


def kernel(
    groups,
    members,
    factor,
    hid_hbm,
    wsh_ref,
    tgt_hbm,
    hg_hbm,
    comb_ref,
    hid_ref,
    tgt_ref,
    hg_ref,
    hid_t,
    w_all,
    term,
    pair,
    hop_in,
    hop_out,
    v_out,
    gath,
    gram_all,
    gram_far,
    gram_sum,
    acc,
    zs,
    zr,
    xs,
    xr,
    ds,
    dr,
    ss,
    sr,
    s2,
    r2,
    hs,
    hr,
    vs,
    vr,
    gs,
    gr,
    ms,
    mr,
    fs,
    fr,
    local,
):
    depth = members // CORES
    half = depth // 2
    rows, width = wsh_ref.shape
    cols = width // groups
    ff = rows * members
    g = lax.axis_index("grp")
    d = lax.axis_index("dp")
    z = d // CORES
    c = d % CORES
    sib = 1 - c
    is_end = (z == 0) | (z == depth - 1)
    end = z // (depth - 1)
    held = end * (half - 1)

    def part(p):
        return pl.ds(p * (rows // PARTS), rows // PARTS)


    def copy(src, dst, send, recv, grp, dp):
        return pltpu.make_async_remote_copy(
            src_ref=src,
            dst_ref=dst,
            send_sem=send,
            recv_sem=recv,
            device_id=(grp, dp),
            device_id_type=pl.DeviceIdType.MESH,
        )

    def col(m):
        return pl.ds(pl.multiple_of(flip(g, m, groups) * cols, 128), cols)

    hid_load = pltpu.make_async_copy(hid_hbm, hid_ref, local.at[0])
    tgt_load = pltpu.make_async_copy(tgt_hbm, tgt_ref, local.at[1])
    hg_store = pltpu.make_async_copy(hg_ref, hg_hbm, local.at[2])

    def own_load(m):
        return pltpu.make_async_copy(wsh_ref.at[:, col(m)], w_all.at[m, d], local.at[3 + m])

    barrier = pltpu.get_barrier_semaphore()
    peers = [(g, flip(z, k, depth) * CORES + c) for k in range(1, depth)]
    peers += [(flip(g, m, groups), d) for m in range(1, groups)]
    peers += [(flip(g, m, groups), z * CORES + sib) for m in range(groups)]
    for grp, dp in peers:
        pl.semaphore_signal(
            barrier, inc=1, device_id=(grp, dp), device_id_type=pl.DeviceIdType.MESH
        )
    pl.semaphore_wait(barrier, len(peers))

    def z_copy(src, way, block):
        target = z - 1 if way == 0 else z + 1
        row = src * CORES + c
        return copy(
            block, w_all.at[0, row], zs.at[way, src], zr.at[src], g, target * CORES + c
        )

    def own_copy(m):
        return copy(
            wsh_ref.at[:, col(m)], w_all.at[m, d], ss.at[m, z], sr.at[m, z], g, z * CORES + sib
        )

    def x_copy(m, src):
        row = src * CORES + c
        return copy(
            w_all.at[0, row], w_all.at[m, row], xs.at[m, src], xr.at[m, src], flip(g, m, groups), d
        )

    def d_copy(side, src):
        side_rows = pl.ds(side * (rows // 2), rows // 2)
        row = src * CORES + c
        return copy(
            w_all.at[1 + side, row, side_rows],
            w_all.at[3, row, side_rows],
            ds.at[side, src],
            dr.at[side, src],
            flip(g, 2 - side, groups),
            d,
        )

    def s_copy(m, src):
        row = src * CORES + c
        return copy(
            w_all.at[m, row], w_all.at[m, row], ss.at[m, src], sr.at[m, src], g, z * CORES + sib
        )

    def at_distance(h, action):
        for way in range(2):
            src = z + h if way == 0 else z - h

            @pl.when((src >= 0) & (src < depth))
            def _():
                action(src, way)

    def sends_on(way):
        return z > 0 if way == 0 else z < depth - 1

    def line_step(src, way):
        z_copy(src, way, wsh_ref.at[:, col(0)]).wait_recv()

        @pl.when(sends_on(way))
        def _():
            z_copy(src, way, w_all.at[0, src * CORES + c]).start()

        x_copy(1, src).start()
        x_copy(2, src).start()
        s_copy(0, src).start()

    def cross_step(src, way):
        for m in (1, 2):
            x_copy(m, src).wait_recv()
            d_copy(m - 1, src).start()
            s_copy(m, src).start()

    def corner_step(src, way):
        for side in range(2):
            d_copy(side, src).wait_recv()
        s_copy(3, src).start()

    for way in range(2):

        @pl.when(sends_on(way))
        def _():
            z_copy(z, way, wsh_ref.at[:, col(0)]).start()

    for m in range(groups):
        own_copy(m).start()
    for m in range(groups):
        own_load(m).start()
    hid_load.start()
    tgt_load.start()
    hid_load.wait()
    hid_t[...] = hid_ref[...].T

    for h in range(1, depth):
        at_distance(h, line_step)
        if 1 <= h - 1 < depth - 2:
            at_distance(h - 1, cross_step)
    tgt_load.wait()
    for m in range(groups):
        own_load(m).wait()

    def pair_copy(s):
        return copy(
            term.at[s, sib], pair.at[s], s2.at[s], r2.at[s], g, z * CORES + sib
        )

    def hop_copy(s, way, j, p):
        target = z - 1 if way == 0 else z + 1
        return copy(
            hop_out.at[s, way, j, part(p)],
            hop_in.at[s, way, j, part(p)],
            hs.at[s, way, j, p],
            hr.at[s, way, j, p],
            g,
            target * CORES + c,
        )

    def v_copy(s, j, p):
        return copy(
            v_out.at[s, j, part(p)],
            gath.at[g, j, part(p)],
            vs.at[s, j, p],
            vr.at[s, j, p],
            flip(g, s, groups),
            d,
        )

    def m_copy(s, j):
        group = flip(g, s, groups)
        return copy(
            gath.at[group, j],
            gath.at[group, 0],
            ms.at[s, j],
            mr.at[s],
            g,
            (end * half + j) * CORES + c,
        )

    def pieces():
        return [(j, p) for j in range(half) for p in range(PARTS)]

    def to_middle(action):
        for j in range(half):

            @pl.when(j != held)
            def _():
                action(j)

    def forward(s):
        @pl.when(s > 0)
        def _():
            for j, p in pieces():
                v_copy(s, j, p).wait_recv()

        to_middle(lambda j: m_copy(s, j).start())

    def chip_sum(s, block, p):
        return term[s, c, block, part(p)].astype(jnp.float32) + pair[s, block, part(p)].astype(
            jnp.float32
        )

    def process(t):
        for way in range(2):
            place = depth - 1 - z if way == 0 else z
            s = t - place
            inside = (s >= 0) & (s < groups)

            @pl.when(inside & (place == 0))
            def _():
                for j, p in pieces():
                    mine = chip_sum(s, way * half + j, p)
                    hop_out[s, way, j, part(p)] = mine.astype(jnp.bfloat16)
                    hop_copy(s, way, j, p).start()

            @pl.when(inside & (place > 0) & (place < depth - 1))
            def _():
                for j, p in pieces():
                    mine = chip_sum(s, way * half + j, p)
                    hop_copy(s, way, j, p).wait_recv()
                    total = mine + hop_in[s, way, j, part(p)].astype(jnp.float32)
                    hop_out[s, way, j, part(p)] = total.astype(jnp.bfloat16)
                    hop_copy(s, way, j, p).start()

            @pl.when(inside & (place == depth - 1))
            def _():
                for j, p in pieces():
                    mine = chip_sum(s, way * half + j, p)
                    hop_copy(s, way, j, p).wait_recv()
                    total = mine + hop_in[s, way, j, part(p)].astype(jnp.float32)
                    final = total.astype(jnp.bfloat16)

                    @pl.when(s == 0)
                    def _():
                        gath[g, j, part(p)] = final

                    @pl.when(s > 0)
                    def _():
                        v_out[s, j, part(p)] = final
                        v_copy(s, j, p).start()

        s1 = t - depth

        @pl.when(is_end & (s1 >= 0) & (s1 < groups - 1))
        def _():
            forward(s1)

    def slot(m, carry):
        @pl.when(m == 1)
        def _():
            for h in range(max(1, depth - 2), depth):
                at_distance(h, cross_step)

        @pl.when(m == 2)
        def _():
            for h in range(1, depth):
                at_distance(h, corner_step)

        for k in range(depth):
            s_copy(m, k).wait_recv()
        weight = w_all[m].reshape(ff, cols)
        output = jnp.dot(hid_ref[...], weight, preferred_element_type=jnp.float32)
        error = (output - tgt_ref[:, col(m)].astype(jnp.float32)).astype(jnp.bfloat16)
        product = jnp.dot(hid_t[...], error, preferred_element_type=jnp.float32)
        product = (product * factor).astype(jnp.bfloat16)
        for i in range(members):
            term[m, i % CORES, i // CORES] = product[i * rows : (i + 1) * rows]
        pair_copy(m).start()
        grad = lax.dot_general(
            error, weight, (((1,), (1,)), ((), ())), preferred_element_type=jnp.float32
        )

        @pl.when(m == 0)
        def _():
            acc[...] = grad

        @pl.when(m > 0)
        def _():
            acc[...] += grad

        pair_copy(m).wait_recv()
        process(m)
        return carry

    lax.fori_loop(0, groups, slot, 0)
    hg_ref[...] = acc[...].astype(jnp.bfloat16)
    hg_store.start()

    def tail(t, carry):
        process(t)
        return carry

    lax.fori_loop(groups, groups + depth - 1, tail, 0)

    pairs = [(i, j) for i in range(groups) for j in range(i, groups)]
    near = [(m, e) for m in range(groups) for e in range(CORES) if m + e > 0]

    def near_copy(n):
        m, e = near[n]
        core = c if e == 0 else sib
        return copy(
            gram_sum,
            gram_all.at[n],
            gs.at[n],
            gr.at[n],
            flip(g, m, groups),
            z * CORES + core,
        )

    def far_copy(k, e):
        return copy(
            gram_far.at[e],
            gram_far.at[e],
            fs.at[k],
            fr.at[e],
            g,
            flip(z, k, depth) * CORES + c,
        )

    @pl.when(is_end)
    def _():
        forward(groups - 1)
        vecs = [gath[i].reshape(half * rows, cols).astype(jnp.float32) for i in range(groups)]
        lines = []
        for i, j in pairs:
            line = jnp.sum(vecs[i] * vecs[j], axis=0, keepdims=True)
            lines.append(sum(line[:, n * 128 : (n + 1) * 128] for n in range(cols // 128)))
        pad = gram_sum.shape[0] - len(lines)
        lines.append(jnp.zeros((pad, 128), jnp.float32))
        mine = jnp.concatenate(lines, axis=0)
        gram_sum[...] = mine
        for n in range(len(near)):
            near_copy(n).start()
        for n in range(len(near)):
            near_copy(n).wait_recv()
        gram_far[end] = mine + jnp.sum(gram_all[...], axis=0)
        for k in range(1, depth):
            far_copy(k, end).start()
        far_copy(1, 1 - end).wait_recv()

    @pl.when(jnp.logical_not(is_end))
    def _():
        for s in range(groups):
            m_copy(s, 0).wait_recv()
        for e in range(2):
            far_copy(1, e).wait_recv()

    total = jnp.sum(gram_far[0] + gram_far[1], axis=1, keepdims=True)
    gram = {ij: total[n : n + 1] for n, ij in enumerate(pairs)}
    coef = group_coefficients(gram, groups)
    comb_ref[...] = sum(coef[i] * gath[i, held].astype(jnp.float32) for i in range(groups))

    @pl.when(is_end)
    def _():
        for s in range(1, groups):
            for j, p in pieces():
                v_copy(s, j, p).wait_send()
        for s in range(groups):
            to_middle(lambda j: m_copy(s, j).wait_send())
        for n in range(len(near)):
            near_copy(n).wait_send()
        for k in range(1, depth):
            far_copy(k, end).wait_send()

    for way in range(2):
        for h in range(depth):
            src = z - h if way else z + h

            @pl.when(sends_on(way) & (src >= 0) & (src < depth))
            def _():
                z_copy(src, way, wsh_ref.at[:, col(0)]).wait_send()

    def cross_done(src, way):
        for m in (1, 2):
            x_copy(m, src).wait_send()
            d_copy(m - 1, src).wait_send()

    for h in range(1, depth):
        at_distance(h, cross_done)
    hg_store.wait()
    for m in range(groups):
        pair_copy(m).wait_send()
        for k in range(depth):
            s_copy(m, k).wait_send()
        for way in range(2):

            @pl.when(z != way * (depth - 1))
            def _():
                for j, p in pieces():
                    hop_copy(m, way, j, p).wait_send()


def put_out(hg_in, comb_in, hg_out, comb_out, hg_buf, comb_buf, sems):
    loads = [
        pltpu.make_async_copy(comb_in, comb_buf, sems.at[0]),
        pltpu.make_async_copy(hg_in, hg_buf, sems.at[1]),
    ]
    stores = [
        pltpu.make_async_copy(comb_buf, comb_out, sems.at[2]),
        pltpu.make_async_copy(hg_buf, hg_out, sems.at[3]),
    ]
    for load in loads:
        load.start()
    for load, store in zip(loads, stores):
        load.wait()
        store.start()
    for store in stores:
        store.wait()


def fused(hidden, weight, target):
    groups = lax.axis_size("grp")
    members = lax.axis_size("dp")
    tokens, ff = hidden.shape
    rows, width = weight.shape
    cols = width // groups
    depth = members // CORES
    half = depth // 2
    factor = 1.0 / math.sqrt(tokens * members)
    bf16, f32 = jnp.bfloat16, jnp.float32
    pads = -(-(groups * (groups + 1) // 2) // 8) * 8 + 8
    near = groups * CORES - 1
    vmem = pl.BlockSpec(memory_space=pltpu.VMEM)
    hbm = pl.BlockSpec(memory_space=pltpu.HBM)
    dma = pltpu.SemaphoreType.DMA
    block = (rows, cols)
    scratch = [
        pltpu.VMEM((tokens, ff), bf16),
        pltpu.VMEM((tokens, width), bf16),
        pltpu.VMEM((tokens, ff), bf16),
        pltpu.VMEM((ff, tokens), bf16),
        pltpu.VMEM((groups, members) + block, bf16),
        pltpu.VMEM((groups, CORES, depth) + block, bf16),
        pltpu.VMEM((groups, depth) + block, bf16),
        pltpu.VMEM((groups, 2, half) + block, bf16),
        pltpu.VMEM((groups, 2, half) + block, bf16),
        pltpu.VMEM((groups, half) + block, bf16),
        pltpu.VMEM((groups, half) + block, bf16),
        pltpu.VMEM((near, pads, 128), f32),
        pltpu.VMEM((2, pads, 128), f32),
        pltpu.VMEM((pads, 128), f32),
        pltpu.VMEM((tokens, ff), f32),
        dma((2, depth)),
        dma((depth,)),
        dma((groups, depth)),
        dma((groups, depth)),
        dma((2, depth)),
        dma((2, depth)),
        dma((groups, depth)),
        dma((groups, depth)),
        dma((groups,)),
        dma((groups,)),
        dma((groups, 2, half, PARTS)),
        dma((groups, 2, half, PARTS)),
        dma((groups, half, PARTS)),
        dma((groups, half, PARTS)),
        dma((near,)),
        dma((near,)),
        dma((groups, half)),
        dma((groups,)),
        dma((depth,)),
        dma((2,)),
        dma((3 + groups,)),
    ]
    results = pl.pallas_call(
        functools.partial(kernel, groups, members, factor),
        out_shape=(
            jax.ShapeDtypeStruct((tokens, ff), bf16),
            jax.ShapeDtypeStruct(block, f32),
        ),
        in_specs=[hbm] * 3,
        out_specs=(hbm, vmem),
        scratch_shapes=scratch,
        compiler_params=pltpu.CompilerParams(
            collective_id=0, has_side_effects=True, vmem_limit_bytes=56 * 2**20
        ),
    )(hidden, weight, target)
    return pl.pallas_call(
        put_out,
        out_shape=tuple(jax.ShapeDtypeStruct(r.shape, r.dtype) for r in results),
        in_specs=[hbm, hbm],
        out_specs=(hbm, hbm),
        scratch_shapes=[
            pltpu.VMEM((tokens, ff), bf16),
            pltpu.VMEM(block, f32),
            dma((4,)),
        ],
    )(*results)


def plain(hidden, weight, target):
    rows = hidden.shape[0]
    members = lax.axis_size("dp")
    factor = 1.0 / math.sqrt(rows * members)
    weight_full = lax.all_gather(weight, "dp", axis=0, tiled=True)
    output = jnp.dot(hidden, weight_full, preferred_element_type=jnp.float32)
    error = (output - target.astype(jnp.float32)).astype(jnp.bfloat16)
    product = lax.dot_general(
        hidden, error, (((0,), (0,)), ((), ())), preferred_element_type=jnp.float32
    )
    shard = lax.psum_scatter(
        (product * factor).astype(jnp.bfloat16), "dp", scatter_dimension=0, tiled=True
    ).astype(jnp.float32)
    hidden_grad = lax.dot_general(
        error, weight_full, (((1,), (1,)), ((), ())), preferred_element_type=jnp.float32
    ).astype(jnp.bfloat16)
    levels = lax.axis_size("grp").bit_length() - 1
    for level in range(levels):
        other = partner(shard.astype(jnp.bfloat16), "grp", level).astype(shard.dtype)
        own_sq, other_sq, cross = lax.psum(
            (jnp.sum(shard * shard), jnp.sum(other * other), jnp.sum(shard * other)), "dp"
        )
        coef_own, coef_other = coefficients(own_sq, other_sq, cross)
        shard = coef_own * shard + coef_other * other
    columns = shard.shape[1] // lax.axis_size("grp")
    mine = lax.dynamic_slice_in_dim(shard, lax.axis_index("grp") * columns, columns, 1)
    return (hidden_grad, mine)


def shards(hidden, weight, target):
    groups, members = lax.axis_size("grp"), lax.axis_size("dp")
    rows, width = weight.shape
    power = all(n & (n - 1) == 0 for n in (groups, members))
    aligned = rows % (16 * PARTS) == 0 and width % (128 * groups) == 0
    if power and aligned and members >= 2 * CORES and groups == 4:
        return fused(hidden, weight, target)
    return plain(hidden, weight, target)


def solution(mesh):
    in_specs = (P(("grp", "dp"), None), P("dp", None), P(("grp", "dp"), None))
    out_specs = (P(("grp", "dp"), None), P("dp", "grp"))
    return jax.shard_map(shards, mesh=mesh, in_specs=in_specs, out_specs=out_specs, check_vma=False)
```
